256 devices in a mesh: dp: 32 (over x_hi, z, core), tensor: 8 (over y, x_lo).
Axes of the slice: x: 4 (x_hi: 2, x_lo: 2; x = x_hi * 2 + x_lo), y: 4, z: 8, core: 2. Of those that a mesh axis runs over, the one named last changes fastest.
Arguments:
- master: float32 [2, 16384, 16384], P(None, ('tensor', 'dp')), may hold values from -0.1875 to 0.1875
- tile_order: int32 [8, 16], P('tensor'), may hold values from 0 to 15, each once within a row
- check_weights: int32 [8, 16384], P(None, 'tensor'), may hold values from -7 to 7
Outputs:
- tiled: bfloat16 [2, 16384, 16384], P(None, 'tensor', 'dp')
- checksum: float32 [2, 8, 16384], P(None, None, ('dp', 'tensor'))
The draws below stay inside these ranges and needn't reach their ends.
Inputs may be any that keep to these rules, and one draw needn't show every extreme that they name: Each row of tile_order lists every number of 0 to 15 once.
All inputs are finite; a program needn't handle non-finite values.
Results may differ from the reference program's by a relative error of at most 0.0029.
Values may be sent and summed in bfloat16 or wider, within the bound.
No kernel may reach another device: no remote copies, remote signals or barrier semaphores. Data moves between devices by JAX's collectives and lax.ppermute only.
A program may use at most 128 MiB of HBM per device.

```python
import jax
import jax.numpy as jnp

D = 16384
LAYERS = 2
TILE = 128
NCHK = 8
GROUPS = 8
TILES_T = 16


def set_ends(values, rng, least, high):
    place = [jax.random.randint(jax.random.fold_in(rng, axis), (), 0, length) for axis, length in enumerate(values.shape)]
    main_axis = values.shape.index(max(values.shape))
    next_to = place[:main_axis] + [(place[main_axis] + 1) % values.shape[main_axis]] + place[main_axis + 1:]
    return values.at[tuple(place)].set(least).at[tuple(next_to)].set(high)


def with_spikes(array, key, source, target, shards_of, factor):
    owner, partner = [(jnp.arange(array.shape[dim]) // (array.shape[dim] // shards_of)).reshape([-1 if axis == dim else 1 for axis in range(array.ndim)]) for dim in (source, target)]
    chosen = jax.random.permutation(key, shards_of)[partner]
    strong = (owner == chosen) | (owner == (partner + shards_of // 2) % shards_of)
    return jnp.where(strong, factor * array, array)


def steps_of(own_key, shape, split, smallest, high):
    gain = 1.0
    for dim, parts in split:
        draws = jax.random.uniform(jax.random.fold_in(jax.random.fold_in(own_key, 6), dim), (parts,), jnp.float32, smallest / len(split), high / len(split))
        gain = gain * jnp.repeat(jnp.exp(draws), shape[dim] // parts).reshape((-1,) + (1,) * (len(shape) - 1 - dim))
    return gain


def bell_draw_with(rng, extent, width, most, split, heavy, dtype=jnp.bfloat16):
    values = width * jax.random.normal(rng, extent, jnp.float32)
    if split:
        values = values * steps_of(rng, extent, split, -0.22, 0.18)
    return jnp.clip(with_spikes(values, jax.random.fold_in(rng, 3), *heavy), -most, most).astype(dtype)


def setup_inputs(seed: int = 0) -> dict:
    arg_keys = jax.random.split(jax.random.key(seed), 4)
    master = bell_draw_with(arg_keys[0], (LAYERS, D, D), D ** -0.5, 0.1875, ((1, 256),), (1, 2, 256, 6.0), jnp.float32)
    tile_order = jax.vmap(lambda own: jax.random.permutation(own, TILES_T))(jax.random.split(arg_keys[1], GROUPS)).reshape((GROUPS, TILES_T)).astype(jnp.int32)
    check_weights = set_ends(jax.random.randint(arg_keys[2], (NCHK, D), -7, 8), jax.random.fold_in(arg_keys[2], 1), -7, 7).astype(jnp.int32)
    return dict(master=master, tile_order=tile_order, check_weights=check_weights)


def reference(master, tile_order, check_weights):
    low = master.astype(jnp.bfloat16)
    blocks = low.reshape(LAYERS, GROUPS, TILES_T, TILE, D)
    index = tile_order.astype(jnp.int32)[None, :, :, None, None]
    moved = jnp.take_along_axis(blocks, index, axis=2)
    tiled = moved.reshape(LAYERS, D, D)
    weights = check_weights.astype(jnp.bfloat16)
    sums = []
    for layer in range(LAYERS):
        sums.append(jnp.dot(weights, tiled[layer], preferred_element_type=jnp.float32))
    checksum = jnp.stack(sums, axis=0)
    return tiled, checksum
```

```python
import functools

import jax
import jax.numpy as jnp
from jax import lax
from jax.experimental import pallas as pl
from jax.experimental.pallas import tpu as pltpu
from jax.sharding import PartitionSpec as P

TILE = 128


def pack_kernel(master_ref, out_ref):
    per_step, layers, rows, columns = out_ref.shape
    for i in range(per_step):
        for l in range(layers):
            block = master_ref[l, :, i * columns:(i + 1) * columns]
            out_ref[i, l] = block.astype(jnp.bfloat16)


def pack(master, parts, per_step):
    layers, rows, width = master.shape
    columns = width // parts
    return pl.pallas_call(
        pack_kernel,
        grid=(parts // per_step,),
        in_specs=[pl.BlockSpec((layers, rows, per_step * columns), lambda i: (0, 0, i))],
        out_specs=pl.BlockSpec((per_step, layers, rows, columns), lambda i: (i, 0, 0, 0)),
        out_shape=jax.ShapeDtypeStruct((parts, layers, rows, columns), jnp.bfloat16),
        name="pack",
    )(master)


def regroup_kernel(order_ref, weights_ref, received_ref, tiled_ref, sums_ref, held, in_sems, out_sems):
    count = in_sems.shape[0]
    parts, layers, rows, columns = held.shape
    halves = parts // count
    groups, _, width = sums_ref.shape

    def fetch(k):
        source = order_ref[k]
        return pltpu.make_async_copy(
            received_ref.at[pl.ds(source * halves, halves)],
            held.at[pl.ds(k * halves, halves)],
            in_sems.at[k],
        )

    def put(k, h, l):
        part = k * halves + h
        return pltpu.make_async_copy(
            held.at[part, l],
            tiled_ref.at[l, pl.ds(part * rows, rows)],
            out_sems.at[k, h, l],
        )

    for k in range(count):
        fetch(k).start()
    sums = [jnp.zeros((weights_ref.shape[0], columns), jnp.float32) for _ in range(layers)]
    for k in range(count):
        fetch(k).wait()
        for h in range(halves):
            for l in range(layers):
                put(k, h, l).start()
        for h in range(halves):
            part = k * halves + h
            weights = weights_ref[:, part * rows:(part + 1) * rows].astype(jnp.float32).astype(jnp.bfloat16)
            for l in range(layers):
                sums[l] += jnp.dot(weights, held[part, l], preferred_element_type=jnp.float32)
    each = width // layers
    for t in range(groups):
        pieces = [sums[l][:, t * each:(t + 1) * each] for l in range(layers)]
        sums_ref[t] = jnp.concatenate(pieces, axis=1)
    for k in range(count):
        for h in range(halves):
            for l in range(layers):
                put(k, h, l).wait()


def regroup(order, weights, received, groups):
    parts, layers, rows, columns = received.shape
    count = order.shape[0]
    halves = parts // count
    checks = weights.shape[0]
    return pl.pallas_call(
        regroup_kernel,
        in_specs=[
            pl.BlockSpec(memory_space=pltpu.SMEM),
            pl.BlockSpec(memory_space=pltpu.VMEM),
            pl.BlockSpec(memory_space=pl.ANY),
        ],
        out_specs=[
            pl.BlockSpec(memory_space=pl.ANY),
            pl.BlockSpec(memory_space=pltpu.VMEM),
        ],
        out_shape=[
            jax.ShapeDtypeStruct((layers, parts * rows, columns), jnp.bfloat16),
            jax.ShapeDtypeStruct((groups, checks, layers * columns // groups), jnp.float32),
        ],
        scratch_shapes=[
            pltpu.VMEM((parts, layers, rows, columns), jnp.bfloat16),
            pltpu.SemaphoreType.DMA((count,)),
            pltpu.SemaphoreType.DMA((count, halves, layers)),
        ],
        name="regroup",
    )(order, weights, received)


def total_kernel(parts_ref, out_ref):
    total = parts_ref[0]
    for t in range(1, parts_ref.shape[0]):
        total += parts_ref[t]
    layers, _, each = out_ref.shape
    for l in range(layers):
        out_ref[l] = total[:, l * each:(l + 1) * each]


def on_device(parts, groups, master, tile_order, check_weights):
    layers = master.shape[0]
    packed = pack(master, parts, 4)
    received = lax.all_to_all(packed, "dp", split_axis=0, concat_axis=0, tiled=True)
    tiled, sums = regroup(tile_order[0], check_weights, received, groups)
    sums = lax.all_to_all(sums, "tensor", split_axis=0, concat_axis=0, tiled=True)
    checks, width = sums.shape[1:]
    checksum = pl.pallas_call(
        total_kernel,
        out_shape=jax.ShapeDtypeStruct((layers, checks, width // layers), jnp.float32),
        name="total",
    )(sums)
    return (tiled, checksum)


def solution(mesh):
    in_specs = (P(None, ("tensor", "dp"), None), P("tensor", None), P(None, "tensor"))
    out_specs = (P(None, "tensor", "dp"), P(None, None, ("dp", "tensor")))
    body = functools.partial(on_device, mesh.shape["dp"], mesh.shape["tensor"])
    return jax.shard_map(body, mesh=mesh, in_specs=in_specs, out_specs=out_specs, check_vma=False)
```

```python
import functools

import jax
import jax.numpy as jnp
from jax import lax
from jax.experimental import pallas as pl
from jax.experimental.pallas import tpu as pltpu
from jax.sharding import PartitionSpec as P


NX, NZ = 2, 8
DIRECT = ((0, 4), (1, 4))
FIRST = ((1, 3), (1, 5), (0, 3), (0, 5))
SECOND = ((1, 2), (1, 6), (0, 2), (0, 6), (1, 0))
THIRD = ((1, 1), (1, 7), (0, 1), (0, 7))
SWAPPED = FIRST + SECOND + THIRD


GRANT = 12 * 2**20
PACK_GRANT = 56 * 2**20


def send(array, delta):
    return lax.ppermute(array, "dp", shift(*delta))


def position():
    me = lax.axis_index("dp")
    core = lax.rem(me, 2)
    chip = me // 2
    return chip // NZ, lax.rem(chip, NZ), core


def device_at(dx, dz, dc):
    x, z, core = position()
    return (lax.rem(x + dx, NX) * NZ + lax.rem(z + dz, NZ)) * 2 + lax.rem(core + dc, 2)


def shift(dx, dz, dc):
    pairs = []
    for x in range(NX):
        for z in range(NZ):
            for core in range(2):
                target = ((x + dx) % NX * NZ + (z + dz) % NZ) * 2 + (core + dc) % 2
                pairs.append(((x * NZ + z) * 2 + core, target))
    return pairs


def pack_kernel(blocks, copies, *refs):
    n_out = 1 + max(out for _, out, _ in blocks)
    master_ref = refs[0]
    swapped_ref = refs[1] if copies else None
    first = 2 if copies else 1
    outs = refs[first:first + n_out]
    wide, low, in_sems, out_sems = refs[first + n_out:]
    layers, _, columns = wide.shape[1:]

    def fetch(i):
        start = pl.multiple_of(device_at(*blocks[i][0]) * columns, columns)
        return pltpu.make_async_copy(master_ref.at[:, :, pl.ds(start, columns)], wide.at[i], in_sems.at[i])

    def fetch_copy(i):
        j = len(blocks) + i
        return pltpu.make_async_copy(swapped_ref.at[copies[i][0]], low.at[j], in_sems.at[j])

    def put(j, out, slot):
        target = outs[out] if slot is None else outs[out].at[slot]
        return pltpu.make_async_copy(low.at[j], target, out_sems.at[j])

    for i in range(len(blocks)):
        fetch(i).start()
    for i in range(len(copies)):
        fetch_copy(i).start()
    for i in range(len(blocks)):
        fetch(i).wait()
        for l in range(layers):
            low[i, l] = wide[i, l].astype(jnp.bfloat16)
        put(i, blocks[i][1], blocks[i][2]).start()
    for i in range(len(copies)):
        fetch_copy(i).wait()
        put(len(blocks) + i, copies[i][1], copies[i][2]).start()
    for i in range(len(blocks)):
        put(i, blocks[i][1], blocks[i][2]).wait()
    for i in range(len(copies)):
        put(len(blocks) + i, copies[i][1], copies[i][2]).wait()


def pack(master, swapped, parts, blocks, copies, shapes):
    layers, rows, width = master.shape
    columns = width // parts
    count = len(blocks) + len(copies)
    operands = (master, swapped) if copies else (master,)
    piece = layers * rows * columns * 2
    return pl.pallas_call(
        functools.partial(pack_kernel, blocks, copies),
        in_specs=[pl.BlockSpec(memory_space=pltpu.HBM)] + [pl.BlockSpec(memory_space=pl.ANY)] * (len(operands) - 1),
        out_specs=[pl.BlockSpec(memory_space=pl.ANY)] * len(shapes),
        out_shape=[jax.ShapeDtypeStruct(s + (layers, rows, columns), jnp.bfloat16) for s in shapes],
        scratch_shapes=[
            pltpu.VMEM((len(blocks), layers, rows, columns), jnp.float32),
            pltpu.VMEM((count, layers, rows, columns), jnp.bfloat16),
            pltpu.SemaphoreType.DMA((count,)),
            pltpu.SemaphoreType.DMA((count,)),
        ],
        cost_estimate=pl.CostEstimate(
            flops=0, transcendentals=0, bytes_accessed=piece * (3 * len(blocks) + 2 * len(copies))
        ),
        compiler_params=pltpu.CompilerParams(vmem_limit_bytes=PACK_GRANT if not copies else GRANT),
    )(*operands)


def regroup_kernel(chips, aliased, groups, *refs):
    order_ref, weights_ref = refs[:2]
    n_in = sum(2 if split else 1 for _, split in chips)
    pieces = refs[2:2 + n_in]
    rest = refs[2 + n_in:]
    sums_in = None
    if aliased:
        sums_in, rest = rest[0], rest[2:]
    tiled_ref, sums_ref, place, held, in_sems, out_sems = rest
    count = order_ref.shape[0]
    layers, tile_rows, columns = held.shape[1:]
    rows = tile_rows // 2
    x, z, core = position()

    for k in range(count):
        place[order_ref[k]] = k

    where = []
    for dx, dz in [delta for delta, _ in chips]:
        chip = lax.rem(x + NX - dx, NX) * NZ + lax.rem(z + NZ - dz, NZ)
        where.append(place[chip])

    copies = []
    at = 0
    for i, (_, split) in enumerate(chips):
        for slot in range(2):
            source = pieces[at + slot] if split else pieces[at].at[slot]
            half = core if slot == 0 else 1 - core
            start = pl.multiple_of(half * rows, rows)
            copies.append(pltpu.make_async_copy(source, held.at[i, :, pl.ds(start, rows)], in_sems.at[i, slot]))
        at += 2 if split else 1

    def put(i, l):
        start = pl.multiple_of(where[i] * tile_rows, tile_rows)
        return pltpu.make_async_copy(held.at[i, l], tiled_ref.at[l, pl.ds(start, tile_rows)], out_sems.at[i, l])

    for copy in copies:
        copy.start()
    checks = weights_ref.shape[0]
    sums = [sums_in[l] if aliased else jnp.zeros((checks, columns), jnp.float32) for l in range(layers)]
    for i in range(len(chips)):
        copies[2 * i].wait()
        copies[2 * i + 1].wait()
        for l in range(layers):
            put(i, l).start()
        start = pl.multiple_of(where[i] * tile_rows, tile_rows)
        weights = weights_ref[:, pl.ds(start, tile_rows)].astype(jnp.float32).astype(jnp.bfloat16)
        for l in range(layers):
            sums[l] += jnp.dot(weights, held[i, l], preferred_element_type=jnp.float32)
    if groups:
        each = columns // groups
        for t in range(groups):
            sums_ref[t] = jnp.concatenate([s[:, t * each:(t + 1) * each] for s in sums], axis=1)
    else:
        for l in range(layers):
            sums_ref[l] = sums[l]
    for i in range(len(chips)):
        for l in range(layers):
            put(i, l).wait()


def regroup(order, weights, pieces, chips, before, groups):
    layers, rows, columns = pieces[0].shape[-3:]
    count = order.shape[0]
    checks, height = weights.shape
    any_space = pl.BlockSpec(memory_space=pl.ANY)
    vmem = pl.BlockSpec(memory_space=pltpu.VMEM)
    specs = [pl.BlockSpec(memory_space=pltpu.SMEM), vmem] + [any_space] * len(pieces)
    operands = [order, weights, *pieces]
    aliases = {}
    if before is not None:
        tiled, sums = before
        operands += [sums, tiled]
        specs += [vmem, pl.BlockSpec(memory_space=pltpu.HBM)]
        aliases = {len(operands) - 1: 0}
    shape = (groups, checks, layers * columns // groups) if groups else (layers, checks, columns)
    n = len(chips)
    hbm = pl.BlockSpec(memory_space=pltpu.HBM)
    return pl.pallas_call(
        functools.partial(regroup_kernel, chips, before is not None, groups),
        in_specs=specs,
        out_specs=[hbm, vmem],
        out_shape=[
            jax.ShapeDtypeStruct((layers, height, columns), jnp.bfloat16),
            jax.ShapeDtypeStruct(shape, jnp.float32),
        ],
        scratch_shapes=[
            pltpu.SMEM((count,), jnp.int32),
            pltpu.VMEM((n, layers, 2 * rows, columns), jnp.bfloat16),
            pltpu.SemaphoreType.DMA((n, 2)),
            pltpu.SemaphoreType.DMA((n, layers)),
        ],
        input_output_aliases=aliases,
        cost_estimate=pl.CostEstimate(
            flops=2 * n * checks * layers * 2 * rows * columns,
            transcendentals=0,
            bytes_accessed=2 * n * layers * 2 * rows * columns * 2,
        ),
        compiler_params=pltpu.CompilerParams(vmem_limit_bytes=GRANT),
    )(*operands)


def total_kernel(parts_ref, out_ref):
    total = parts_ref[0]
    for t in range(1, parts_ref.shape[0]):
        total += parts_ref[t]
    layers, _, each = out_ref.shape
    for l in range(layers):
        out_ref[l] = total[:, l * each:(l + 1) * each]


def on_device(parts, groups, master, tile_order, check_weights):
    layers = master.shape[0]
    order = tile_order[0]

    blocks = tuple((delta + (dc,), 2 * i + dc, None) for i, delta in enumerate(DIRECT) for dc in range(2))
    direct = pack(master, None, parts, blocks, (), [()] * len(blocks))
    direct = [send(a, b[0]) for a, b in zip(direct, blocks)]

    mine = ((0, 0),) + SWAPPED
    blocks = tuple((delta + (1,), 0, i) for i, delta in enumerate(mine))
    (sibling,) = pack(master, None, parts, blocks, (), [(len(mine),)])
    swapped = send(sibling, (0, 0, 1))

    blocks = tuple((delta + (0,), i, 0) for i, delta in enumerate(mine))
    copies = tuple((i, i, 1) for i in range(len(mine)))
    pieces = pack(master, swapped, parts, blocks, copies, [(2,)] * len(mine))
    here, pieces = pieces[0], pieces[1:]
    moved = {d: send(a, d + (0,)) for d, a in zip(SWAPPED, pieces)}

    chips = (((0, 0), False),) + tuple((d, True) for d in DIRECT) + tuple((d, False) for d in FIRST)
    state = regroup(order, check_weights, [here, *direct, *(moved[d] for d in FIRST)], chips, None, 0)
    chips = tuple((d, False) for d in SECOND)
    state = regroup(order, check_weights, [moved[d] for d in SECOND], chips, state, 0)
    chips = tuple((d, False) for d in THIRD)
    tiled, sums = regroup(order, check_weights, [moved[d] for d in THIRD], chips, state, groups)

    sums = lax.all_to_all(sums, "tensor", split_axis=0, concat_axis=0, tiled=True)
    checks, width = sums.shape[1:]
    checksum = pl.pallas_call(
        total_kernel,
        out_shape=jax.ShapeDtypeStruct((layers, checks, width // layers), jnp.float32),
        name="total",
    )(sums)
    return (tiled, checksum)


def solution(mesh):
    in_specs = (P(None, ("tensor", "dp"), None), P("tensor", None), P(None, "tensor"))
    out_specs = (P(None, "tensor", "dp"), P(None, None, ("dp", "tensor")))

    def body(*args):
        return on_device(mesh.shape["dp"], mesh.shape["tensor"], *args)

    return jax.shard_map(body, mesh=mesh, in_specs=in_specs, out_specs=out_specs, check_vma=False)
```

```python
import functools

import jax
import jax.numpy as jnp
from jax import lax
from jax.experimental import pallas as pl
from jax.experimental.pallas import tpu as pltpu
from jax.sharding import PartitionSpec as P


NX, NZ = 2, 8
DIRECT = ((0, 4), (1, 4))
FIRST = ((1, 3), (1, 5), (0, 3), (0, 5))
SECOND = ((1, 2), (1, 6), (0, 2), (0, 6))
THIRD = ((1, 0), (1, 1), (1, 7), (0, 1), (0, 7))
EXTRA = 8
GRANT = 12 * 2**20
PACK_GRANT = 50 * 2**20

VMEM = pl.BlockSpec(memory_space=pltpu.VMEM)
SMEM = pl.BlockSpec(memory_space=pltpu.SMEM)
HBM = pl.BlockSpec(memory_space=pltpu.HBM)
ANY = pl.BlockSpec(memory_space=pl.ANY)


def send(array, delta):
    return lax.ppermute(array, "dp", shift(*delta))


def exchange(array):
    return lax.all_to_all(array, "tensor", split_axis=0, concat_axis=0, tiled=True)


def position():
    me = lax.axis_index("dp")
    core = lax.rem(me, 2)
    chip = me // 2
    return chip // NZ, lax.rem(chip, NZ), core


def device_at(dx, dz, dc):
    x, z, core = position()
    return (lax.rem(x + dx, NX) * NZ + lax.rem(z + dz, NZ)) * 2 + lax.rem(core + dc, 2)


def sender(dx, dz):
    x, z, _ = position()
    return lax.rem(x + NX - dx, NX) * NZ + lax.rem(z + NZ - dz, NZ)


def shift(dx, dz, dc):
    pairs = []
    for x in range(NX):
        for z in range(NZ):
            for core in range(2):
                target = ((x + dx) % NX * NZ + (z + dz) % NZ) * 2 + (core + dc) % 2
                pairs.append(((x * NZ + z) * 2 + core, target))
    return pairs


def place_of(order_ref, place):
    for k in range(order_ref.shape[0]):
        place[order_ref[k]] = k


def tile_weights(weights_ref, k, tile_rows):
    start = pl.multiple_of(k * tile_rows, tile_rows)
    weights = weights_ref[:, pl.ds(start, tile_rows)].astype(jnp.float32)
    half = tile_rows // 2
    turned = jnp.concatenate([weights[:, half:], weights[:, :half]], axis=1)
    core = position()[2]
    return jnp.where(core == 0, weights, turned).astype(jnp.bfloat16)


def by_owner(sums, groups):
    each = sums[0].shape[1] // groups
    return [jnp.concatenate([s[:, t * each:(t + 1) * each] for s in sums], axis=1) for t in range(groups)]


def pack_kernel(blocks, copies, n_out, summed, *refs):
    refs = list(refs)
    master_ref = refs.pop(0)
    swapped_ref = refs.pop(0) if copies else None
    if summed:
        order_ref, weights_ref = refs.pop(0), refs.pop(0)
    outs, refs = refs[:n_out], refs[n_out:]
    if summed:
        sums_ref = refs.pop(0)
        place = refs.pop()
    wide, sems = refs
    layers, rows, columns = wide.shape[1:]

    def fetch(i):
        start = pl.multiple_of(device_at(*blocks[i][0]) * columns, columns)
        return pltpu.make_async_copy(master_ref.at[:, :, pl.ds(start, columns)], wide.at[i], sems.at[i])

    for i in range(len(blocks)):
        fetch(i).start()
    for source, out, offset, stride in copies:
        for l in range(layers):
            outs[out][offset + l * stride:offset + l * stride + rows] = swapped_ref[source, l]
    if summed:
        place_of(order_ref, place)
        x, z, _ = position()
        weights = tile_weights(weights_ref, place[x * NZ + z], 2 * rows)
    done = 0
    for i, (_, out, offset, stride) in enumerate(blocks):
        fetch(i).wait()
        for l in range(layers):
            low = wide[i, l].astype(jnp.bfloat16)
            if isinstance(offset, tuple):
                outs[out][offset[0], l] = low
            else:
                outs[out][offset + l * stride:offset + l * stride + rows] = low
        if out in summed:
            tile = [outs[out][l * 2 * rows:(l + 1) * 2 * rows] for l in range(layers)]
            sums = [jnp.dot(weights, t, preferred_element_type=jnp.float32) for t in tile]
            for t, part in enumerate(by_owner(sums, sums_ref.shape[0])):
                sums_ref[t, done] = part
            done += 1


def pack(master, parts, blocks, shapes, swapped=None, copies=(), summed=(), checks=None, grant=PACK_GRANT):
    layers, rows, width = master.shape
    columns = width // parts
    operands, specs = [master], [HBM]
    if copies:
        operands.append(swapped)
        specs.append(VMEM)
    out_shape = [jax.ShapeDtypeStruct(s, jnp.bfloat16) for s in shapes]
    scratch = [
        pltpu.VMEM((len(blocks), layers, rows, columns), jnp.float32),
        pltpu.SemaphoreType.DMA((len(blocks),)),
    ]
    flops = 0
    if summed:
        order, weights, groups = checks
        operands += [order, weights]
        specs += [SMEM, VMEM]
        out_shape.append(
            jax.ShapeDtypeStruct((groups, len(summed), weights.shape[0], layers * columns // groups), jnp.float32)
        )
        scratch.append(pltpu.SMEM((order.shape[0],), jnp.int32))
        flops = 2 * len(summed) * weights.shape[0] * layers * 2 * rows * columns
    piece = layers * rows * columns * 2
    return pl.pallas_call(
        functools.partial(pack_kernel, blocks, copies, len(shapes), summed),
        in_specs=specs,
        out_specs=[VMEM] * len(out_shape),
        out_shape=out_shape,
        scratch_shapes=scratch,
        cost_estimate=pl.CostEstimate(
            flops=flops, transcendentals=0, bytes_accessed=piece * (3 * len(blocks) + 2 * len(copies))
        ),
        compiler_params=pltpu.CompilerParams(vmem_limit_bytes=grant),
    )(*operands)


def put_tile(piece, tiled_ref, k, layers, rows, sems, split):
    core = position()[2]
    copies = []
    for slot in range(2):
        half = core if slot == 0 else 1 - core
        start = pl.multiple_of(k * 2 * rows + half * rows, rows)
        for l in range(layers):
            at = l * rows if split else (2 * l + slot) * rows
            source = piece[slot if split else 0].at[pl.ds(at, rows)]
            target = tiled_ref.at[l, pl.ds(start, rows)]
            copies.append(pltpu.make_async_copy(source, target, sems.at[slot, l]))
    return copies


def regroup_kernel(chips, aliased, groups, rows, *refs):
    refs = list(refs)
    order_ref, weights_ref = refs.pop(0), refs.pop(0)
    pieces = []
    for _, split in chips:
        pieces.append([refs.pop(0) for _ in range(2 if split else 1)])
    if aliased:
        sums_in = refs.pop(0)
        refs.pop(0)
    tiled_ref, sums_ref, place, sems = refs
    layers, _, columns = tiled_ref.shape
    place_of(order_ref, place)
    where = [place[sender(*delta)] for delta, _ in chips]
    copies = []
    for i, (_, split) in enumerate(chips):
        copies += put_tile(pieces[i], tiled_ref, where[i], layers, rows, sems.at[i], split)
    for copy in copies:
        copy.start()
    checks = weights_ref.shape[0]
    sums = [sums_in[l] if aliased else jnp.zeros((checks, columns), jnp.float32) for l in range(layers)]
    for i, (_, split) in enumerate(chips):
        weights = tile_weights(weights_ref, where[i], 2 * rows)
        for l in range(layers):
            if split:
                for slot in range(2):
                    sums[l] += jnp.dot(
                        weights[:, slot * rows:(slot + 1) * rows],
                        pieces[i][slot][l * rows:(l + 1) * rows],
                        preferred_element_type=jnp.float32,
                    )
            else:
                sums[l] += jnp.dot(
                    weights, pieces[i][0][2 * l * rows:2 * (l + 1) * rows], preferred_element_type=jnp.float32
                )
    if groups:
        for t, part in enumerate(by_owner(sums, groups)):
            sums_ref[t] = part
    else:
        for l in range(layers):
            sums_ref[l] = sums[l]
    for copy in copies:
        copy.wait()


def regroup(order, weights, pieces, chips, shape, before, groups):
    layers, height, columns = shape
    count = order.shape[0]
    checks = weights.shape[0]
    rows = height // count // 2
    operands = [order, weights, *pieces]
    specs = [SMEM, VMEM] + [VMEM] * len(pieces)
    aliases = {}
    if before is not None:
        tiled, sums = before
        operands += [sums, tiled]
        specs += [VMEM, HBM]
        aliases = {len(operands) - 1: 0}
    sums_shape = (groups, checks, layers * columns // groups) if groups else (layers, checks, columns)
    n = len(chips)
    return pl.pallas_call(
        functools.partial(regroup_kernel, chips, before is not None, groups, rows),
        in_specs=specs,
        out_specs=[HBM, VMEM],
        out_shape=[jax.ShapeDtypeStruct(shape, jnp.bfloat16), jax.ShapeDtypeStruct(sums_shape, jnp.float32)],
        scratch_shapes=[pltpu.SMEM((count,), jnp.int32), pltpu.SemaphoreType.DMA((n, 2, layers))],
        input_output_aliases=aliases,
        cost_estimate=pl.CostEstimate(
            flops=2 * n * checks * layers * 2 * rows * columns,
            transcendentals=0,
            bytes_accessed=2 * n * layers * 2 * rows * columns * 2,
        ),
        compiler_params=pltpu.CompilerParams(vmem_limit_bytes=GRANT),
    )(*operands)


def attach_kernel(parts_ref, *refs):
    n = parts_ref.shape[1]
    outs = refs[n:2 * n]
    extra, sems = refs[2 * n:]
    copies = []
    for i in range(n):
        total = parts_ref[0, i]
        for g in range(1, parts_ref.shape[0]):
            total += parts_ref[g, i]
        high = total.astype(jnp.bfloat16)
        rest = total - high.astype(jnp.float32)
        middle = rest.astype(jnp.bfloat16)
        low = (rest - middle.astype(jnp.float32)).astype(jnp.bfloat16)
        extra[i] = jnp.concatenate([high, middle, low, jnp.zeros_like(low)], axis=1)
        height = outs[i].shape[0]
        copies.append(pltpu.make_async_copy(extra.at[i], outs[i].at[pl.ds(height - EXTRA, EXTRA)], sems.at[i]))
        copies[-1].start()
    for copy in copies:
        copy.wait()


def attach(parts, pieces):
    n = len(pieces)
    return pl.pallas_call(
        attach_kernel,
        in_specs=[VMEM] + [ANY] * n,
        out_specs=[ANY] * n,
        out_shape=[jax.ShapeDtypeStruct(p.shape, p.dtype) for p in pieces],
        scratch_shapes=[pltpu.VMEM((n, EXTRA, pieces[0].shape[1]), jnp.bfloat16), pltpu.SemaphoreType.DMA((n,))],
        input_output_aliases={i + 1: i for i in range(n)},
        compiler_params=pltpu.CompilerParams(vmem_limit_bytes=GRANT),
        cost_estimate=pl.CostEstimate(flops=0, transcendentals=0, bytes_accessed=parts.size * 4),
        name="attach",
    )(parts, *pieces)


def finish_kernel(chips, rows, *refs):
    refs = list(refs)
    order_ref, parts_ref = refs.pop(0), refs.pop(0)
    pieces, refs = refs[:len(chips)], refs[len(chips) + 1:]
    tiled_ref, checksum_ref, place, sems = refs
    layers = tiled_ref.shape[0]
    place_of(order_ref, place)
    copies = []
    for i, delta in enumerate(chips):
        copies += put_tile([pieces[i]], tiled_ref, place[sender(*delta)], layers, rows, sems.at[i], False)
    for copy in copies:
        copy.start()
    total = parts_ref[0]
    for g in range(1, parts_ref.shape[0]):
        total += parts_ref[g]
    width = total.shape[1]
    for piece in pieces:
        extra = piece[piece.shape[0] - EXTRA:].astype(jnp.float32)
        total += extra[:, :width] + (extra[:, width:2 * width] + extra[:, 2 * width:3 * width])
    each = width // layers
    for l in range(layers):
        checksum_ref[l] = total[:, l * each:(l + 1) * each]
    for copy in copies:
        copy.wait()


def finish(order, parts, pieces, chips, tiled):
    layers, height, _ = tiled.shape
    count = order.shape[0]
    rows = height // count // 2
    _, checks, width = parts.shape
    n = len(chips)
    return pl.pallas_call(
        functools.partial(finish_kernel, chips, rows),
        in_specs=[SMEM, VMEM] + [VMEM] * n + [HBM],
        out_specs=[HBM, VMEM],
        out_shape=[
            jax.ShapeDtypeStruct(tiled.shape, tiled.dtype),
            jax.ShapeDtypeStruct((layers, checks, width // layers), jnp.float32),
        ],
        scratch_shapes=[pltpu.SMEM((count,), jnp.int32), pltpu.SemaphoreType.DMA((n, 2, layers))],
        input_output_aliases={2 + n: 0},
        compiler_params=pltpu.CompilerParams(vmem_limit_bytes=GRANT),
        name="finish",
    )(order, parts, *pieces, tiled)


def on_device(parts, groups, master, tile_order, check_weights):
    layers, rows, width = master.shape
    columns = width // parts
    order = tile_order[0]
    shape = (layers, check_weights.shape[1], columns)
    whole = (layers * 2 * rows, columns)
    longer = (layers * 2 * rows + EXTRA, columns)

    blocks = tuple((d + (dc,), 2 * i + dc, 0, rows) for i, d in enumerate(DIRECT) for dc in range(2))
    direct = pack(master, parts, blocks, [(layers * rows, columns)] * len(blocks))
    direct = [send(a, b[0]) for a, b in zip(direct, blocks)]

    mine = FIRST + ((0, 0),) + SECOND + THIRD
    blocks = tuple((d + (1,), 0, (i,), 0) for i, d in enumerate(mine))
    (sibling,) = pack(master, parts, blocks, [(len(mine), layers, rows, columns)])
    swapped = send(sibling, (0, 0, 1))

    n = len(FIRST)
    blocks = tuple((d + (0,), i, 0, 2 * rows) for i, d in enumerate(FIRST))
    copies = tuple((i, i, rows, 2 * rows) for i in range(n))
    first = pack(master, parts, blocks, [whole] * n, swapped, copies)
    first = [send(a, d + (0,)) for d, a in zip(FIRST, first)]

    rest = mine[n:]
    blocks = tuple((d + (0,), i, 0, 2 * rows) for i, d in enumerate(rest))
    copies = tuple((n + i, i, rows, 2 * rows) for i in range(len(rest)))
    shapes = [whole] * (1 + len(SECOND)) + [longer] * len(THIRD)
    summed = tuple(range(1 + len(SECOND), len(rest)))
    here, *rest, sums = pack(master, parts, blocks, shapes, swapped, copies, summed, (order, check_weights, groups))
    second = [send(a, d + (0,)) for d, a in zip(SECOND, rest)]
    late = attach(exchange(sums), rest[len(SECOND):])
    third = [send(a, d + (0,)) for d, a in zip(THIRD, late)]

    chips = (((0, 0), False),) + tuple((d, True) for d in DIRECT) + tuple((d, False) for d in FIRST)
    state = regroup(order, check_weights, [here, *direct, *first], chips, shape, None, 0)
    chips = tuple((d, False) for d in SECOND)
    tiled, sums = regroup(order, check_weights, second, chips, shape, state, groups)
    return tuple(finish(order, exchange(sums), third, THIRD, tiled))


def solution(mesh):
    in_specs = (P(None, ("tensor", "dp"), None), P("tensor", None), P(None, "tensor"))
    out_specs = (P(None, "tensor", "dp"), P(None, None, ("dp", "tensor")))

    def body(*args):
        return on_device(mesh.shape["dp"], mesh.shape["tensor"], *args)

    return jax.shard_map(body, mesh=mesh, in_specs=in_specs, out_specs=out_specs, check_vma=False)
```
